768 devices in a mesh: dp: 48 (over z, y_hi), row: 4 (over x), col: 4 (over y_lo, core).
Axes of the slice: x: 4, y: 8 (y_hi: 4, y_lo: 2; y = y_hi * 2 + y_lo), z: 12, core: 2. Of those that a mesh axis runs over, the one named last changes fastest.
Arguments:
- inputs: float32 [12288, 6144], P('dp', 'row'), may hold values from -6 to 6
- out_grad: float32 [12288, 2048], P('dp', 'col'), may hold values from -6 to 6
- weight: float32 [6144, 2048], P(('row', 'dp'), 'col'), may hold values from -0.078125 to 0.078125
- moment_mean: float32 [6144, 2048], P(('row', 'dp'), 'col'), may hold values from -6 to 6
- moment_square: float32 [6144, 2048], P(('row', 'dp'), 'col'), may hold values from 0.5 to 2
Outputs:
- outputs: float32 [12288, 2048], P(('dp', 'row'), 'col')
- in_grad: float32 [12288, 6144], P(('dp', 'col'), 'row')
- new_weight: float32 [6144, 2048], P(('row', 'dp'), 'col')
- new_mean: float32 [6144, 2048], P(('row', 'dp'), 'col')
- new_square: float32 [6144, 2048], P(('row', 'dp'), 'col')
The draws below stay inside these ranges and needn't reach their ends.
All inputs are finite; a program needn't handle non-finite values.
Results may differ from the reference program's by a relative error of at most 0.00007.
Values sent between devices are 32-bit elements; how exact they have to be, the bound alone decides.
A program may use at most 32 MiB of HBM per device.

```python
import math
import jax
import jax.numpy as jnp
from jax import lax

DIN = 6144
DOUT = 2048
STEP = 10
TOKENS = 12288


def block_scale(stream_key, dims, pieces, least, largest):
    loudness = 1.0
    for axis_at, parts in pieces:
        steps = jax.random.uniform(jax.random.fold_in(jax.random.fold_in(stream_key, 6), axis_at), (parts,), jnp.float32, least / len(pieces), largest / len(pieces))
        loudness = loudness * jnp.repeat(jnp.exp(steps), dims[axis_at] // parts).reshape((-1,) + (1,) * (len(dims) - 1 - axis_at))
    return loudness


def normal_values(rng, extent, spread, reach, pieces=(), held_as=jnp.bfloat16):
    array = spread * jax.random.normal(rng, extent, jnp.float32)
    if pieces:
        array = array * block_scale(rng, extent, pieces, -0.22, 0.18)
    return jnp.clip(array, -reach, reach).astype(held_as)


def setup_inputs(seed: int = 0) -> dict:
    key_list = jax.random.split(jax.random.key(seed), 6)
    return {
        "inputs": normal_values(key_list[0], (TOKENS, DIN), 1.0, 6.0, ((0, 48), (1, 4)), jnp.float32),
        "out_grad": normal_values(key_list[1], (TOKENS, DOUT), 1.0, 6.0, ((0, 48), (1, 4)), jnp.float32),
        "weight": normal_values(key_list[2], (DIN, DOUT), DIN ** -0.5, 0.078125, ((0, 192), (1, 4)), jnp.float32),
        "moment_mean": normal_values(key_list[3], (DIN, DOUT), 1.0, 6.0, ((0, 192), (1, 4)), jnp.float32),
        "moment_square": jnp.clip(jnp.exp(math.log(2.0) - 1.3862944 * jax.random.uniform(key_list[4], (DIN, DOUT), jnp.float32) ** block_scale(key_list[4], (DIN, DOUT), ((0, 192), (1, 4)), -0.2, 0.2)), 0.5, 2.0),
    }


def adamw_update(weight, moment_mean, moment_square, gradient):
    new_mean = 0.9 * moment_mean + 0.1 * gradient
    new_square = 0.95 * moment_square + 0.05 * gradient * gradient
    mean_hat = new_mean / (1.0 - 0.9 ** STEP)
    square_hat = new_square / (1.0 - 0.95 ** STEP)
    new_weight = weight - 0.02 * (mean_hat / (jnp.sqrt(square_hat) + 1e-08) + 0.1 * weight)
    return (new_weight, new_mean, new_square)

def reference(inputs, out_grad, weight, moment_mean, moment_square):
    highest = lax.Precision.HIGHEST
    outputs = jnp.dot(inputs, weight, precision=highest, preferred_element_type=jnp.float32)
    in_grad = lax.dot_general(out_grad, weight, (((1,), (1,)), ((), ())), precision=highest, preferred_element_type=jnp.float32)
    gradient = lax.dot_general(inputs, out_grad, (((0,), (0,)), ((), ())), precision=highest, preferred_element_type=jnp.float32)
    gradient = gradient * (1.0 / math.sqrt(TOKENS))
    new_weight, new_mean, new_square = adamw_update(weight, moment_mean, moment_square, gradient)
    return (outputs, in_grad, new_weight, new_mean, new_square)
```

```python
import math

import jax
import jax.numpy as jnp
from jax import lax
from jax.experimental import pallas as pl
from jax.experimental.pallas import tpu as pltpu
from jax.sharding import Mesh
from jax.sharding import PartitionSpec as P

STEP = 10
NZ, NH, NX = 12, 4, 4
HALF = NZ // 2
ORDER = (0, 1, 3, 2)
LAST = ((0, 1), (3, 2))
MESH = pl.DeviceIdType.MESH
ROWS = 32
SLAB = NH * ROWS
F32 = jnp.float32
BF16 = jnp.bfloat16


def halves(value):
    high = value.astype(BF16)
    low = (value - high.astype(F32)).astype(BF16)
    return high, low


def dot3(a, b, dims):
    (ah, al), (bh, bl) = a, b

    def one(p, q):
        return lax.dot_general(p, q, (dims, ((), ())), preferred_element_type=F32)

    return one(ah, bh) + (one(ah, bl) + one(al, bh))


def kernel(
    in_ref, og_ref, w_ref, mm_ref, ms_ref,
    out_ref, ig_ref, nw_ref, nm_ref, ns_ref,
    wt, rs, first, prod, total, hland, pout, xland, pin, cland, yland,
    in_hi, in_lo, og_hi, og_lo,
    h_s, h_r, ag_s, ag_r, rs_s, rs_r, c_s, c_r, y_s, y_r, x_s, x_r, g_s, g_r,
):
    z, h, x = lax.axis_index("z"), lax.axis_index("h"), lax.axis_index("x")
    l, c = lax.axis_index("l"), lax.axis_index("c")

    def around(at, by, n):
        return lax.rem(at + by + n, n)

    def to(axis, at, by, n):
        return {axis: around(at, by, n)}

    def copy(src, dst, s, r, dev):
        return pltpu.make_async_remote_copy(
            src_ref=src, dst_ref=dst, send_sem=s, recv_sem=r, device_id=dev, device_id_type=MESH
        )

    partners = [to("z", z, 1, NZ), to("z", z, -1, NZ), {"c": 1 - c}, {"l": 1 - l}]
    partners += [to("h", h, j, NH) for j in (1, 2, 3)] + [to("x", x, j, NX) for j in (1, 2, 3)]
    barrier = pltpu.get_barrier_semaphore()
    for dev in partners:
        pl.semaphore_signal(barrier, inc=1, device_id=dev, device_id_type=MESH)
    pl.semaphore_wait(barrier, len(partners))

    def rows_of(zz, hh):
        return pl.ds(pl.multiple_of((zz * NH + hh) * ROWS, ROWS), ROWS)

    def slab_at(zz):
        return pl.ds(pl.multiple_of(zz * SLAB, SLAB), SLAB)

    def sign(d):
        return 1 - 2 * d

    def h_copy(j):
        return copy(w_ref, wt.at[rows_of(z, h)], h_s.at[j - 1], h_r.at[j - 1], to("h", h, j, NH))

    def ag_copy(d, i, k, src=None):
        zz = around(z, -sign(d) * i, NZ)
        here = wt.at[rows_of(zz, around(h, -k, NH))]
        return copy(here if src is None else src, here, ag_s.at[d, i, k], ag_r.at[d, i, k], to("z", z, sign(d), NZ))

    for d in (0, 1):
        ag_copy(d, 0, 0, w_ref).start()
    for j in (1, 3, 2):
        h_copy(j).start()
    wt[rows_of(z, h), :] = w_ref[...]

    og_hi[...], og_lo[...] = halves(og_ref[...])
    in_hi[...], in_lo[...] = halves(in_ref[...])
    og = lambda: (og_hi[...], og_lo[...])

    def product(zz):
        a = (in_hi[:, slab_at(zz)], in_lo[:, slab_at(zz)])
        return dot3(a, og(), ((0,), (0,)))

    def rs_copy(d, i, half, src):
        rows = pl.ds(half * 64, 64)
        return copy(src.at[rows], rs.at[d, i, rows], rs_s.at[d, i, half], rs_r.at[d, i, half], to("z", z, sign(d), NZ))

    first[...] = product(around(z, HALF, NZ))
    rs_copy(0, 0, 0, first).start()
    rs_copy(1, 0, 1, first).start()

    for k in (1, 3, 2):
        h_copy(k).wait_recv()
        for d in (0, 1):
            ag_copy(d, 0, k).start()

    def c_copy(zz):
        return copy(pin.at[zz, :, 1 - c], cland.at[zz], c_s.at[zz], c_r.at[zz], {"c": 1 - c})

    def y_copy(zz):
        return copy(pin.at[zz, 1 - l, c], yland.at[zz], y_s.at[zz], y_r.at[zz], {"l": 1 - l})

    def slab(zz, start):
        w = halves(wt[slab_at(zz), :])
        part = dot3(og(), w, ((1,), (1,)))
        pin[zz] = part.reshape(2, 2, 64, 128)
        c_copy(zz).start()
        out = dot3((in_hi[:, slab_at(zz)], in_lo[:, slab_at(zz)]), w, ((1,), (0,)))
        pout[...] = out if start else pout[...] + out

    def second(zz):
        c_copy(zz).wait_recv()
        c_copy(zz).wait_send()
        pin[zz, 1 - l, c] = pin[zz, 1 - l, c] + cland[zz, 1 - l]
        y_copy(zz).start()

    for d in (0, 1):
        prod[d] = product(around(z, sign(d) * (HALF - 1), NZ))
    slab(z, True)

    def tick(i, carry):
        for k in ORDER:
            for d in (0, 1):
                ag_copy(d, i - 1, k).wait_recv()
                if k in LAST[d]:
                    ag_copy(d, i, k).start()
                else:

                    @pl.when(i < HALF - 1)
                    def _():
                        ag_copy(d, i, k).start()

        for half in (0, 1):
            for d in (0, 1):
                rows = pl.ds(half * 64, 64)

                def add():
                    rs_copy(d, i - 1, half, first).wait_recv()
                    rs[d, i - 1, rows, :] = rs[d, i - 1, rows, :] + prod[d, rows, :]

                if half == d:
                    add()
                else:
                    pl.when(i > 1)(add)

                    @pl.when(i == 1)
                    def _():
                        rs[d, i - 1, rows, :] = prod[d, rows, :]

                rs_copy(d, i, half, rs.at[d, i - 1]).start()

        def each(d, carry):
            @pl.when(jnp.logical_or(i > 1, d == 0))
            def _():
                second(around(z, sign(d) * (1 - i), NZ))

            slab(around(z, -sign(d) * i, NZ), False)
            prod[d] = product(around(z, sign(d) * (HALF - 1 - i), NZ))
            return carry

        return lax.fori_loop(0, 2, each, carry)

    lax.fori_loop(1, HALF, tick, 0)

    far = around(z, HALF, NZ)
    for d in (0, 1):
        for k in LAST[d]:
            ag_copy(d, HALF - 1, k).wait_recv()
    slab(far, False)

    def x_copy(j):
        at = pl.ds(pl.multiple_of(around(x, j, NX) * 64, 64), 64)
        return copy(pout.at[at], xland.at[j - 1], x_s.at[j - 1], x_r.at[j - 1], to("x", x, j, NX))

    for j in (2, 1, 3):
        x_copy(j).start()

    for half in (0, 1):
        rows = pl.ds(half * 64, 64)
        for d in (0, 1):
            rs_copy(d, HALF - 1, half, first).wait_recv()
        total[rows, :] = prod[0, rows, :] + rs[0, HALF - 1, rows, :] + rs[1, HALF - 1, rows, :]

    def g_copy(j):
        at = pl.ds(pl.multiple_of(around(h, j, NH) * ROWS, ROWS), ROWS)
        return copy(total.at[at], hland.at[j - 1], g_s.at[j - 1], g_r.at[j - 1], to("h", h, j, NH))

    for j in (2, 1, 3):
        g_copy(j).start()

    second(around(z, 1 - HALF, NZ))
    second(around(z, HALF - 1, NZ))
    second(far)

    def finish(zz, carry):
        y_copy(zz).wait()
        at = pl.ds(pl.multiple_of(zz * 128, 128), 128)
        ig_ref[:, at] = pin[zz, l, c] + cland[zz, l] + yland[zz]
        return carry

    lax.fori_loop(0, NZ, finish, 0)

    for j in (1, 2, 3):
        x_copy(j).wait()
    out_ref[...] = (
        pout[pl.ds(pl.multiple_of(x * 64, 64), 64), :] + xland[0] + (xland[1] + xland[2])
    )

    for j in (1, 2, 3):
        g_copy(j).wait()
    summed = total[pl.ds(pl.multiple_of(h * ROWS, ROWS), ROWS), :] + hland[0] + (hland[1] + hland[2])
    gradient = summed * (1.0 / math.sqrt(NZ * NH * 256))
    new_mean = 0.9 * mm_ref[...] + 0.1 * gradient
    new_square = 0.95 * ms_ref[...] + 0.05 * gradient * gradient
    mean_hat = new_mean / (1.0 - 0.9**STEP)
    square_hat = new_square / (1.0 - 0.95**STEP)
    weight = w_ref[...]
    nw_ref[...] = weight - 0.02 * (mean_hat / (jnp.sqrt(square_hat) + 1e-08) + 0.1 * weight)
    nm_ref[...] = new_mean
    ns_ref[...] = new_square

    for j in (1, 2, 3):
        h_copy(j).wait_send()

    def drain(i, carry):
        for d in (0, 1):
            for k in ORDER:
                if k in LAST[d]:
                    ag_copy(d, i, k).wait_send()
                else:

                    @pl.when(i < HALF - 1)
                    def _():
                        ag_copy(d, i, k).wait_send()

            for half in (0, 1):

                def done():
                    rs_copy(d, i, half, first).wait_send()

                if half == d:
                    done()
                else:
                    pl.when(i > 0)(done)
        return carry

    lax.fori_loop(0, HALF, drain, 0)


def per_device(inputs, out_grad, weight, moment_mean, moment_square):
    dma = pltpu.SemaphoreType.DMA
    shape = jax.ShapeDtypeStruct
    vmem = pl.BlockSpec(memory_space=pltpu.VMEM)
    small = shape((ROWS, 512), F32)
    return pl.pallas_call(
        kernel,
        out_shape=(shape((64, 512), F32), shape((64, 1536), F32), small, small, small),
        in_specs=[vmem] * 5,
        out_specs=[vmem] * 5,
        scratch_shapes=[
            pltpu.VMEM((1536, 512), F32),
            pltpu.VMEM((2, HALF, SLAB, 512), F32),
            pltpu.VMEM((SLAB, 512), F32),
            pltpu.VMEM((2, SLAB, 512), F32),
            pltpu.VMEM((SLAB, 512), F32),
            pltpu.VMEM((3, ROWS, 512), F32),
            pltpu.VMEM((256, 512), F32),
            pltpu.VMEM((3, 64, 512), F32),
            pltpu.VMEM((NZ, 2, 2, 64, 128), F32),
            pltpu.VMEM((NZ, 2, 64, 128), F32),
            pltpu.VMEM((NZ, 64, 128), F32),
            pltpu.VMEM((256, 1536), BF16),
            pltpu.VMEM((256, 1536), BF16),
            pltpu.VMEM((256, 512), BF16),
            pltpu.VMEM((256, 512), BF16),
            dma((3,)), dma((3,)),
            dma((2, HALF, 4)), dma((2, HALF, 4)),
            dma((2, HALF, 2)), dma((2, HALF, 2)),
            dma((NZ,)), dma((NZ,)),
            dma((NZ,)), dma((NZ,)),
            dma((3,)), dma((3,)),
            dma((3,)), dma((3,)),
        ],
        compiler_params=pltpu.CompilerParams(
            collective_id=0, has_side_effects=True, vmem_limit_bytes=48 << 20
        ),
        name="step",
    )(inputs, out_grad, weight, moment_mean, moment_square)


def solution(mesh):
    split = Mesh(mesh.devices.reshape(NZ, NH, NX, 2, 2), ("z", "h", "x", "l", "c"))
    tile = P(("x", "z", "h"), ("l", "c"))
    return jax.shard_map(
        per_device,
        mesh=split,
        in_specs=(P(("z", "h"), "x"), P(("z", "h"), ("l", "c")), tile, tile, tile),
        out_specs=(P(("z", "h", "x"), ("l", "c")), P(("z", "h", "l", "c"), "x"), tile, tile, tile),
        check_vma=False,
    )
```

```python
import math

import jax
import jax.numpy as jnp
from jax import lax
from jax.experimental import pallas as pl
from jax.experimental.pallas import tpu as pltpu
from jax.sharding import Mesh
from jax.sharding import PartitionSpec as P

STEP = 10
NZ, NH, NX = 12, 4, 4
HALF = NZ // 2
ORDER = (0, 1, 3, 2)
LAST = ((0, 1), (3, 2))
MESH = pl.DeviceIdType.MESH
ROWS = 32
SLAB = NH * ROWS
COLS = 512
CA = 384
CB = COLS - CA
COPIES = 160
F32 = jnp.float32
BF16 = jnp.bfloat16


def halves(value):
    high = value.astype(BF16)
    low = (value - high.astype(F32)).astype(BF16)
    return high, low


def dot3(a, b, dims):
    (ah, al), (bh, bl) = a, b

    def one(p, q):
        return lax.dot_general(p, q, (dims, ((), ())), preferred_element_type=F32)

    return one(ah, bh) + (one(ah, bl) + one(al, bh))


def sign(d):
    return 1 - 2 * d


def place(d, i):
    return 1 + 4 * ((i - 1) // 2) + 2 * d + (i - 1) % 2


def kernel(
    in_hbm, og_hbm, w_hbm, mm_hbm, ms_hbm,
    out_hbm, ig_hbm, nw_hbm, nm_hbm, ns_hbm,
    out_ref, ig_ref, nw_ref, nm_ref, ns_ref,
    w0, wa, wb, pa, pb, rs, far_l, near_l, q, zb, total, tg, ga, pout, tx, xl, pin, cland, yland,
    in_v, og_v, w_v, mm_v, ms_v, in_hi, in_lo, og_hi, og_lo,
    l_sem, o_sem, s_sem, r_sem, c_s, c_r, y_s, y_r,
):
    z, h, x = lax.axis_index("z"), lax.axis_index("h"), lax.axis_index("x")
    l, c = lax.axis_index("l"), lax.axis_index("c")

    def around(at, by, n):
        return lax.rem(at + by + n, n)

    def zto(by):
        return {"z": around(z, by, NZ)}

    def hto(by):
        return {"h": around(h, by, NH)}

    def xto(by):
        return {"x": around(x, by, NX)}

    def remote(src, dst, s, r, dev):
        return pltpu.make_async_remote_copy(
            src_ref=src, dst_ref=dst, send_sem=s, recv_sem=r, device_id=dev, device_id_type=MESH
        )

    made = []

    def copy(src, dst, dev):
        made.append(remote(src, dst, s_sem.at[len(made)], r_sem.at[len(made)], dev))
        return made[-1]

    loads = [
        pltpu.make_async_copy(a, b, l_sem.at[n])
        for n, (a, b) in enumerate(
            ((w_hbm, w_v), (og_hbm, og_v), (in_hbm, in_v), (mm_hbm, mm_v), (ms_hbm, ms_v))
        )
    ]
    for load in loads:
        load.start()

    partners = [zto(1), zto(-1), {"c": 1 - c}, {"l": 1 - l}]
    partners += [hto(j) for j in (1, 2, 3)] + [xto(j) for j in (1, -1)]
    barrier = pltpu.get_barrier_semaphore()
    for dev in partners:
        pl.semaphore_signal(barrier, inc=1, device_id=dev, device_id_type=MESH)
    pl.semaphore_wait(barrier, len(partners))

    def zz_at(by):
        return around(z, by, NZ)

    def rows_of(hh):
        return pl.ds(pl.multiple_of(hh * ROWS, ROWS), ROWS)

    def lanes_of(zz):
        return pl.ds(pl.multiple_of(zz * SLAB, SLAB), SLAB)

    cols_a, cols_b = pl.ds(0, CA), pl.ds(CA, CB)

    own_h = {j: copy(w_hbm, w0.at[rows_of(h)], hto(j)) for j in (1, 3, 2)}
    ag = {}
    for i in range(HALF):
        for d in (0, 1):
            zz = zz_at(-sign(d) * i)
            for k in ORDER:
                if i < HALF - 1 or k in LAST[d]:
                    at = rows_of(around(h, -k, NH))
                    src = wa.at[zz, at]
                    if i == 0:
                        src = w_hbm.at[:, cols_a] if k == 0 else w0.at[at, cols_a]
                    ag[d, i, k] = copy(src, wa.at[zz, at], zto(sign(d)))

    bz = {}
    for i in range(HALF):
        for d in (0, 1):
            if i < HALF - 1 or d == 0:
                src = w_hbm.at[:, cols_b] if i == 0 else wb.at[h, place(d, i)]
                bz[d, i] = copy(src, wb.at[h, place(d, i + 1)], zto(sign(d)))
    bh, bf = {}, {}
    for b in range(3):
        n = 4 if b < 2 else 3
        for d in (0, 1):
            at = pl.ds(1 + 4 * b, n)
            bh[b, d] = copy(wb.at[h, at], wb.at[h, at], hto(sign(d)))
            at = pl.ds(1 + 4 * b + 2 * d, 2 if d == 0 else n - 2)
            back = around(h, -sign(d), NH)
            bf[b, d] = copy(wb.at[back, at], wb.at[back, at], hto(sign(d)))

    def bhop(i):
        for d in (0, 1):
            if (d, i - 1) in bz:
                bz[d, i - 1].wait_recv()
                if (d, i) in bz:
                    bz[d, i].start()

    rsa = {}
    for i in range(HALF):
        for d in (0, 1):
            for half in (0, 1):
                if i > 0 or half == d:
                    at = pl.ds(half * 64, 64)
                    src = pa.at[0, at] if i == 0 else rs.at[d, i - 1, at]
                    rsa[d, i, half] = copy(src, rs.at[d, i, at], zto(sign(d)))

    groups = (pl.ds(0, HALF), pl.ds(HALF, HALF))
    two = around(h, 2, NH)
    g_far = {d: copy(pb.at[two, groups[d]], far_l.at[d], hto(sign(d))) for d in (0, 1)}
    g_near = {}
    for d in (0, 1):
        to = around(h, sign(d), NH)
        for g in (0, 1):
            g_near[d, g] = copy(pb.at[to, groups[g]], near_l.at[d, groups[g]], hto(sign(d)))
    rz = {}
    for j in range(HALF):
        for d in (0, 1):
            if j >= d:
                src = q.at[0 if d == 0 else NZ - 1] if j == d else zb.at[d, j - 1]
                rz[d, j] = copy(src, zb.at[d, j], zto(sign(d)))

    def rhop(j):
        for d in (0, 1):
            if j < d:
                continue
            if j > d:
                rz[d, j - 1].wait_recv()
                zb[d, j - 1] = zb[d, j - 1] + q[j if d == 0 else NZ - j]
            rz[d, j].start()

    for d in (0, 1):
        ag[d, 0, 0].start()
        bz[d, 0].start()
    for j in (1, 3, 2):
        own_h[j].start()

    for load in loads[:3]:
        load.wait()
    w0[rows_of(h), :] = w_v[...]
    og_hi[...], og_lo[...] = halves(og_v[...])
    in_hi[...], in_lo[...] = halves(in_v[...])

    def og():
        return og_hi[...], og_lo[...]

    def product(s):
        at = lanes_of(zz_at(HALF - s))
        part = dot3((in_hi[:, at], in_lo[:, at]), og(), ((0,), (0,)))
        pa[s] = part[:, :CA]
        pb[:, s] = part[:, CA:].reshape(NH, ROWS, CB)

    def c_copy(zz):
        return remote(pin.at[zz, :, 1 - c], cland.at[zz], c_s.at[zz], c_r.at[zz], {"c": 1 - c})

    def y_copy(zz):
        return remote(pin.at[zz, 1 - l, c], yland.at[zz], y_s.at[zz], y_r.at[zz], {"l": 1 - l})

    def multiply(zz, tile, start):
        w = halves(tile)
        part = dot3(og(), w, ((1,), (1,)))
        pin[zz] = part.reshape(2, 2, 64, 128)
        c_copy(zz).start()
        at = lanes_of(zz)
        out = dot3((in_hi[:, at], in_lo[:, at]), w, ((1,), (0,)))
        pout[...] = out if start else pout[...] + out

    def slab(by, at):
        zz = zz_at(by)
        tile = jnp.concatenate([wa[zz], wb[:, at].reshape(SLAB, CB)], axis=1)
        multiply(zz, tile, False)

    def slabs(first, last):
        def each(n, carry):
            i, d = first + n // 2, n % 2
            slab((2 * d - 1) * i, 1 + 4 * ((i - 1) // 2) + 2 * d + (i - 1) % 2)
            return carry

        lax.fori_loop(0, 2 * (last - first + 1), each, 0)

    def second(zz):
        c_copy(zz).wait_recv()
        c_copy(zz).wait_send()
        pin[zz, 1 - l, c] = pin[zz, 1 - l, c] + cland[zz, 1 - l]
        y_copy(zz).start()

    def seconds(first, last):
        def each(n, carry):
            second(zz_at((2 * (n % 2) - 1) * (first + n // 2)))
            return carry

        lax.fori_loop(0, 2 * (last - first + 1), each, 0)

    def ag_step(i, k):
        for d in (0, 1):
            if (d, i - 1, k) in ag:
                ag[d, i - 1, k].wait_recv()
                if (d, i, k) in ag:
                    ag[d, i, k].start()

    def rs_step(i):
        for half in (0, 1):
            for d in (0, 1):
                at = pl.ds(half * 64, 64)
                mine = pa[i if d == 0 else NZ - i, at, :]
                if (d, i - 1, half) in rsa:
                    rsa[d, i - 1, half].wait_recv()
                    rs[d, i - 1, at, :] = rs[d, i - 1, at, :] + mine
                else:
                    rs[d, i - 1, at, :] = mine
                rsa[d, i, half].start()

    product(0)
    rsa[0, 0, 0].start()
    rsa[1, 0, 1].start()
    for n, k in enumerate((1, 3, 2)):
        own_h[k].wait_recv()
        for d in (0, 1):
            ag[d, 0, k].start()
        product(1 + n)
        product(NZ - 1 - n)
    bhop(1)
    ag_step(1, 0)
    ag_step(1, 1)
    product(4)
    product(8)
    ag_step(1, 3)
    ag_step(1, 2)
    rs_step(1)
    bhop(2)
    for d in (0, 1):
        bh[0, d].start()
    product(5)
    product(7)
    product(6)
    for d in (0, 1):
        g_far[d].start()
    for d in (0, 1):
        g_near[d, 1 - d].start()
    multiply(z, w0[...], True)

    for i in range(2, HALF):
        if i <= 3:
            bhop(2 * i - 1)
        if i <= 4:
            for d in (0, 1):
                bh[i - 2, d].wait_recv()
                bf[i - 2, d].start()
        if i == 3:
            for d in (0, 1):
                for g in (0, 1):
                    g_near[d, g].wait_recv()
            g_near[0, 0].wait_send()
            g_near[1, 1].wait_send()
            q[...] = pb[h] + near_l[0] + near_l[1]
        if i >= 3:
            rhop(2 * (i - 3))
        for k in ORDER:
            ag_step(i, k)
        rs_step(i)
        if i == 2:
            for d in (0, 1):
                g_far[d].wait_recv()
                to = around(h, sign(d), NH)
                pb[to, groups[d]] = pb[to, groups[d]] + far_l[d]
                g_near[d, d].start()
        if i <= 3:
            bhop(2 * i)
            for d in (0, 1):
                bh[i - 1, d].start()
        if i >= 3:
            rhop(2 * (i - 3) + 1)
            for d in (0, 1):
                bf[i - 3, d].wait_recv()
        if i == 3:
            second(z)
            slabs(1, 2)
        if i == 4:
            seconds(1, 2)
            slabs(3, 4)
        if i == 5:
            seconds(3, 4)
            slabs(5, 5)

    for k in ORDER:
        ag_step(HALF, k)
    slab(HALF, place(0, HALF))

    def block(by):
        return pl.ds(pl.multiple_of(around(x, by, NX) * 64, 64), 64)

    sides = (pl.ds(0, 256), pl.ds(256, 256))
    x_far = {d: copy(pout.at[block(2), sides[d]], tx.at[d], xto(sign(d))) for d in (0, 1)}
    x_near = {}
    for d in (0, 1):
        for g in (0, 1):
            x_near[d, g] = copy(
                pout.at[block(sign(d)), sides[g]], xl.at[d, :, sides[g]], xto(sign(d))
            )
    for d in (0, 1):
        x_far[d].start()
    for d in (0, 1):
        x_near[d, 1 - d].start()

    for half in (0, 1):
        at = pl.ds(half * 64, 64)
        for d in (0, 1):
            rsa[d, HALF - 1, half].wait_recv()
        total[at, :] = pa[HALF, at, :] + rs[0, HALF - 1, at, :] + rs[1, HALF - 1, at, :]

    def part_of(by, g):
        return pl.ds(pl.multiple_of(around(h, by, NH) * ROWS + g * 16, 16), 16)

    t_far = {d: copy(total.at[part_of(2, d)], tg.at[d], hto(sign(d))) for d in (0, 1)}
    t_near = {}
    for d in (0, 1):
        for g in (0, 1):
            t_near[d, g] = copy(
                total.at[part_of(sign(d), g)], ga.at[d, pl.ds(g * 16, 16)], hto(sign(d))
            )
    for d in (0, 1):
        t_far[d].start()
    for d in (0, 1):
        t_near[d, 1 - d].start()

    far = zz_at(HALF)
    seconds(5, 5)
    second(far)

    for d in (0, 1):
        x_far[d].wait_recv()
        pout[block(sign(d)), sides[d]] = pout[block(sign(d)), sides[d]] + tx[d]
        x_near[d, d].start()
    for d in (0, 1):
        t_far[d].wait_recv()
        total[part_of(sign(d), d), :] = total[part_of(sign(d), d), :] + tg[d]
        t_near[d, d].start()

    def finish(zz, carry):
        y_copy(zz).wait()
        at = lanes_of(zz)
        ig_ref[:, at] = pin[zz, l, c] + cland[zz, l] + yland[zz]
        return carry

    lax.fori_loop(0, NZ, finish, 0)
    stores = [
        pltpu.make_async_copy(a, b, o_sem.at[n])
        for n, (a, b) in enumerate(
            ((ig_ref, ig_hbm), (out_ref, out_hbm), (nw_ref, nw_hbm), (nm_ref, nm_hbm), (ns_ref, ns_hbm))
        )
    ]
    stores[0].start()
    for load in loads[3:]:
        load.wait()

    def adamw(cols, summed):
        gradient = summed * (1.0 / math.sqrt(NZ * NH * 256))
        new_mean = 0.9 * mm_v[:, cols] + 0.1 * gradient
        new_square = 0.95 * ms_v[:, cols] + 0.05 * gradient * gradient
        mean_hat = new_mean / (1.0 - 0.9**STEP)
        square_hat = new_square / (1.0 - 0.95**STEP)
        weight = w_v[:, cols]
        nw_ref[:, cols] = weight - 0.02 * (mean_hat / (jnp.sqrt(square_hat) + 1e-08) + 0.1 * weight)
        nm_ref[:, cols] = new_mean
        ns_ref[:, cols] = new_square

    for d in (0, 1):
        rz[d, HALF - 1].wait_recv()
    adamw(cols_b, q[HALF] + zb[0, HALF - 1] + zb[1, HALF - 1])

    for d in (0, 1):
        for g in (0, 1):
            x_near[d, g].wait_recv()
    out_ref[...] = pout[block(0), :] + xl[0] + xl[1]
    stores[1].start()

    for d in (0, 1):
        for g in (0, 1):
            t_near[d, g].wait_recv()
    adamw(cols_a, total[rows_of(h), :] + ga[0] + ga[1])
    for store in stores[2:]:
        store.start()

    for one in made:
        if one is not g_near[0, 0] and one is not g_near[1, 1]:
            one.wait_send()
    for store in stores:
        store.wait()


def write(*refs):
    srcs, dsts, held, l_sem, o_sem = refs[:5], refs[5:10], refs[10:15], refs[15], refs[16]
    loads = [pltpu.make_async_copy(a, b, l_sem.at[n]) for n, (a, b) in enumerate(zip(srcs, held))]
    stores = [pltpu.make_async_copy(a, b, o_sem.at[n]) for n, (a, b) in enumerate(zip(held, dsts))]
    for load in loads:
        load.start()
    for load, store in zip(loads, stores):
        load.wait()
        store.start()
    for store in stores:
        store.wait()


def per_device(inputs, out_grad, weight, moment_mean, moment_square):
    dma = pltpu.SemaphoreType.DMA
    shape = jax.ShapeDtypeStruct
    hbm = pl.BlockSpec(memory_space=pl.ANY)
    small = shape((ROWS, COLS), F32)
    results = (shape((64, COLS), F32), shape((64, 1536), F32), small, small, small)

    def f32(*dims):
        return pltpu.VMEM(dims, F32)

    staged = [f32(*result.shape) for result in results]

    done = pl.pallas_call(
        kernel,
        out_shape=results,
        in_specs=[hbm] * 5,
        out_specs=[hbm] * 5,
        scratch_shapes=[
            *staged,
            f32(SLAB, COLS),
            f32(NZ, SLAB, CA),
            f32(NH, 12, ROWS, CB),
            f32(NZ, SLAB, CA),
            f32(NH, NZ, ROWS, CB),
            f32(2, HALF, SLAB, CA),
            f32(2, HALF, ROWS, CB),
            f32(2, NZ, ROWS, CB),
            f32(NZ, ROWS, CB),
            f32(2, HALF, ROWS, CB),
            f32(SLAB, CA),
            f32(2, 16, CA),
            f32(2, ROWS, CA),
            f32(256, COLS),
            f32(2, 64, 256),
            f32(2, 64, COLS),
            f32(NZ, 2, 2, 64, 128),
            f32(NZ, 2, 64, 128),
            f32(NZ, 64, 128),
            f32(256, 1536), f32(256, COLS), f32(ROWS, COLS), f32(ROWS, COLS), f32(ROWS, COLS),
            pltpu.VMEM((256, 1536), BF16),
            pltpu.VMEM((256, 1536), BF16),
            pltpu.VMEM((256, COLS), BF16),
            pltpu.VMEM((256, COLS), BF16),
            dma((5,)), dma((5,)),
            dma((COPIES,)), dma((COPIES,)),
            dma((NZ,)), dma((NZ,)),
            dma((NZ,)), dma((NZ,)),
        ],
        compiler_params=pltpu.CompilerParams(
            collective_id=0, has_side_effects=True, vmem_limit_bytes=67043328
        ),
        name="step",
    )(inputs, out_grad, weight, moment_mean, moment_square)
    return pl.pallas_call(
        write,
        out_shape=results,
        in_specs=[hbm] * 5,
        out_specs=[hbm] * 5,
        scratch_shapes=[*staged, dma((5,)), dma((5,))],
        compiler_params=pltpu.CompilerParams(vmem_limit_bytes=67043328),
        name="write",
    )(*done)


def solution(mesh):
    split = Mesh(mesh.devices.reshape(NZ, NH, NX, 2, 2), ("z", "h", "x", "l", "c"))
    tile = P(("x", "z", "h"), ("l", "c"))
    return jax.shard_map(
        per_device,
        mesh=split,
        in_specs=(P(("z", "h"), "x"), P(("z", "h"), ("l", "c")), tile, tile, tile),
        out_specs=(P(("z", "h", "x"), ("l", "c")), P(("z", "h", "l", "c"), "x"), tile, tile, tile),
        check_vma=False,
    )
```

```python
import math

import jax
import jax.numpy as jnp
from jax import lax
from jax.experimental import pallas as pl
from jax.experimental.pallas import tpu as pltpu
from jax.sharding import Mesh
from jax.sharding import PartitionSpec as P

STEP = 10
NZ, NH, NX = 12, 4, 4
HALF = NZ // 2
MESH = pl.DeviceIdType.MESH
ROWS = 32
SLAB = NH * ROWS
COLS = 512
CA = 384
CB = COLS - CA
ARRIVALS = 103
SENDS = 11
F32 = jnp.float32
BF16 = jnp.bfloat16


def halves(value):
    high = value.astype(BF16)
    low = (value - high.astype(F32)).astype(BF16)
    return high, low


def dot3(a, b, dims):
    (ah, al), (bh, bl) = a, b

    def one(p, q):
        return lax.dot_general(p, q, (dims, ((), ())), preferred_element_type=F32)

    return one(ah, bh) + (one(ah, bl) + one(al, bh))


def sign(d):
    return 1 - 2 * d


def place(d, i):
    return 1 + 4 * ((i - 1) // 2) + 2 * d + (i - 1) % 2


def kernel(
    in_hbm, og_hbm, w_hbm, mm_hbm, ms_hbm,
    out_hbm, ig_hbm, nw_hbm, nm_hbm, ns_hbm,
    out_ref, ig_ref, nw_ref, nm_ref, ns_ref,
    w0, wa, wb, pa, pb, rs, far_l, near_l, q, zb, total, tg, ga, pout, tx, xl, pin, cland, yland,
    in_v, og_v, w_v, mm_v, ms_v, in_hi, in_lo, og3,
    l_sem, o_sem, s_sem, r_sem, c_r, y_r,
):
    z, h, x = lax.axis_index("z"), lax.axis_index("h"), lax.axis_index("x")
    l, c = lax.axis_index("l"), lax.axis_index("c")

    def around(at, by, n):
        return lax.rem(at + by + n, n)

    def zto(by):
        return {"z": around(z, by, NZ)}

    def hto(by):
        return {"h": around(h, by, NH)}

    def xto(by):
        return {"x": around(x, by, NX)}

    def remote(src, dst, s, r, dev):
        return pltpu.make_async_remote_copy(
            src_ref=src, dst_ref=dst, send_sem=s, recv_sem=r, device_id=dev, device_id_type=MESH
        )

    arrivals = []

    def arrival():
        arrivals.append(len(arrivals))
        return arrivals[-1]

    H_SENT, A_SENT, B_SENT, BH_SENT, R_SENT, G_SENT, Q_SENT, X_SENT, T_SENT, C_SENT, Y_SENT = range(SENDS)

    def copy(src, dst, dev, sent, at=None):
        return remote(src, dst, s_sem.at[sent], r_sem.at[arrival() if at is None else at], dev)

    loads = [
        pltpu.make_async_copy(a, b, l_sem.at[n])
        for n, (a, b) in enumerate(
            ((w_hbm, w_v), (og_hbm, og_v), (in_hbm, in_v), (mm_hbm, mm_v), (ms_hbm, ms_v))
        )
    ]
    for load in loads:
        load.start()

    partners = [zto(1), zto(-1), {"c": 1 - c}, {"l": 1 - l}]
    partners += [hto(j) for j in (1, 2, 3)] + [xto(j) for j in (1, -1)]
    barrier = pltpu.get_barrier_semaphore()
    for dev in partners:
        pl.semaphore_signal(barrier, inc=1, device_id=dev, device_id_type=MESH)
    pl.semaphore_wait(barrier, len(partners))

    def zz_at(by):
        return around(z, by, NZ)

    def rows_of(hh):
        return pl.ds(pl.multiple_of(hh * ROWS, ROWS), ROWS)

    def lanes_of(zz):
        return pl.ds(pl.multiple_of(zz * SLAB, SLAB), SLAB)

    cols_a, cols_b = pl.ds(0, CA), pl.ds(CA, CB)

    own_h = {j: copy(w_hbm, w0.at[rows_of(h)], hto(j), H_SENT) for j in (1, 3, 2)}
    ag, came = {}, {}
    for d in (0, 1):
        for k in range(NH):
            at = rows_of(around(h, -k, NH))
            src = w_hbm.at[:, cols_a] if k == 0 else w0.at[at, cols_a]
            ids = arrival()
            came[d] = ids - k
            ag[d, 0, k] = copy(src, wa.at[z, at], zto(sign(d)), A_SENT, ids)
    near_half = h // 2

    def half_of(r):
        return pl.ds(pl.multiple_of((near_half if r == 0 else 1 - near_half) * 64, 64), 64)

    for i in range(1, HALF):
        for d in (0, 1):
            for r in (0, 1):
                if i < HALF - 1 or r == d:
                    here = wa.at[zz_at(-sign(d) * i), half_of(r)]
                    ag[d, i, r] = copy(here, here, zto(sign(d)), A_SENT)

    bz = {}
    for i in range(HALF):
        for d in (0, 1):
            if i < HALF - 1 or d == 0:
                src = w_hbm.at[:, cols_b] if i == 0 else wb.at[h, place(d, i)]
                bz[d, i] = copy(src, wb.at[h, place(d, i + 1)], zto(sign(d)), B_SENT)
    bh, bf = {}, {}
    for b in range(3):
        n = 4 if b < 2 else 3
        for d in (0, 1):
            at = pl.ds(1 + 4 * b, n)
            bh[b, d] = copy(wb.at[h, at], wb.at[h, at], hto(sign(d)), BH_SENT)
            at = pl.ds(1 + 4 * b + 2 * d, 2 if d == 0 else n - 2)
            back = around(h, -sign(d), NH)
            bf[b, d] = copy(wb.at[back, at], wb.at[back, at], hto(sign(d)), BH_SENT)

    def bhop(i):
        for d in (0, 1):
            if (d, i - 1) in bz:
                bz[d, i - 1].wait_recv()
                if (d, i) in bz:
                    bz[d, i].start()

    rsa = {}
    for i in range(HALF):
        for d in (0, 1):
            for half in (0, 1):
                if i > 0 or half == d:
                    at = pl.ds(half * 64, 64)
                    src = pa.at[0, at] if i == 0 else rs.at[d, i - 1, at]
                    rsa[d, i, half] = copy(src, rs.at[d, i, at], zto(sign(d)), R_SENT)

    groups = (pl.ds(0, HALF), pl.ds(HALF, HALF))
    two = around(h, 2, NH)
    g_far = {d: copy(pb.at[two, groups[d]], far_l.at[d], hto(sign(d)), G_SENT) for d in (0, 1)}
    g_near = {}
    for d in (0, 1):
        to = around(h, sign(d), NH)
        for g in (0, 1):
            g_near[d, g] = copy(pb.at[to, groups[g]], near_l.at[d, groups[g]], hto(sign(d)), G_SENT)
    rz = {}
    for j in range(HALF):
        for d in (0, 1):
            if j >= d:
                src = q.at[0 if d == 0 else NZ - 1] if j == d else zb.at[d, j - 1]
                rz[d, j] = copy(src, zb.at[d, j], zto(sign(d)), Q_SENT)

    def rhop(j):
        for d in (0, 1):
            if j < d:
                continue
            if j > d:
                rz[d, j - 1].wait_recv()
                zb[d, j - 1] = zb[d, j - 1] + q[j if d == 0 else NZ - j]
            rz[d, j].start()

    for d in (0, 1):
        ag[d, 0, 0].start()
        bz[d, 0].start()
    for j in (1, 3, 2):
        own_h[j].start()

    for load in loads[:3]:
        load.wait()
    w0[rows_of(h), :] = w_v[...]
    high, low = halves(og_v[...])
    og3[...] = jnp.concatenate([high, high, low], axis=1)
    in_hi[...], in_lo[...] = halves(in_v[...])

    def og():
        return og3[:, :COLS], og3[:, 2 * COLS :]

    def product(s):
        at = lanes_of(zz_at(HALF - s))
        part = dot3((in_hi[:, at], in_lo[:, at]), og(), ((0,), (0,)))
        pa[s] = part[:, :CA]
        pb[:, s] = part[:, CA:].reshape(NH, ROWS, CB)

    def c_copy(zz):
        return remote(pin.at[zz, :, 1 - c], cland.at[zz], s_sem.at[C_SENT], c_r.at[zz], {"c": 1 - c})

    def y_copy(zz):
        return remote(pin.at[zz, 1 - l, c], yland.at[zz], s_sem.at[Y_SENT], y_r.at[0], {"l": 1 - l})

    def multiply(parts, start=False):
        across, down, left = [], [], []
        for zz, tile in parts:
            high, low = halves(tile)
            at = lanes_of(zz)
            across.append(jnp.concatenate([high, low, high], axis=1))
            down += [high, low, high]
            left += [in_hi[:, at], in_hi[:, at], in_lo[:, at]]
        part = lax.dot_general(
            og3[...], jnp.concatenate(across, axis=0), (((1,), (1,)), ((), ())), preferred_element_type=F32
        )
        for n, (zz, _) in enumerate(parts):
            pin[zz] = part[:, n * SLAB : (n + 1) * SLAB].reshape(2, 2, 64, SLAB)
            c_copy(zz).start()
        out = jnp.dot(
            jnp.concatenate(left, axis=1), jnp.concatenate(down, axis=0), preferred_element_type=F32
        )
        pout[...] = out if start else pout[...] + out

    def tile_of(zz, at):
        return jnp.concatenate([wa[zz], wb[:, at].reshape(SLAB, CB)], axis=1)

    def pair(i):
        both = [zz_at(-sign(d) * i) for d in (0, 1)]
        multiply([(zz, tile_of(zz, place(d, i))) for d, zz in enumerate(both)])

    def second(zz):
        c_copy(zz).wait_recv()
        pin[zz, 1 - l, c] = pin[zz, 1 - l, c] + cland[zz, 1 - l]
        y_copy(zz).start()

    def seconds(first, last):
        def each(n, carry):
            second(zz_at((2 * (n % 2) - 1) * (first + n // 2)))
            return carry

        lax.fori_loop(0, 2 * (last - first + 1), each, 0)

    def ag_step(i, r):
        for d in (0, 1):
            if i == 1:
                odd = h % 2
                for k in (0, 3 - 2 * odd) if r == 0 else (1 + 2 * odd, 2):
                    piece = wa.at[z, rows_of(0)]
                    remote(piece, piece, s_sem.at[A_SENT], r_sem.at[came[d] + k], zto(1)).wait_recv()
            elif (d, i - 1, r) in ag:
                ag[d, i - 1, r].wait_recv()
            if (d, i, r) in ag and i > 0:
                ag[d, i, r].start()

    def rs_step(i):
        for half in (0, 1):
            for d in (0, 1):
                at = pl.ds(half * 64, 64)
                mine = pa[i if d == 0 else NZ - i, at, :]
                if (d, i - 1, half) in rsa:
                    rsa[d, i - 1, half].wait_recv()
                    rs[d, i - 1, at, :] = rs[d, i - 1, at, :] + mine
                else:
                    rs[d, i - 1, at, :] = mine
                rsa[d, i, half].start()

    def both(copies):
        for d in (0, 1):
            copies[d].start()

    def over_h(b):
        for d in (0, 1):
            bh[b, d].wait_recv()
            bf[b, d].start()

    def piece(k):
        own_h[k].wait_recv()
        for d in (0, 1):
            ag[d, 0, k].start()

    product(0)
    rsa[0, 0, 0].start()
    rsa[1, 0, 1].start()
    bhop(1)
    product(1)
    product(NZ - 1)
    piece(1)
    product(2)
    product(NZ - 2)
    bhop(2)
    for d in (0, 1):
        bh[0, d].start()
    piece(3)
    product(3)
    product(NZ - 3)
    rs_step(1)
    product(4)
    product(NZ - 4)
    product(5)
    product(NZ - 5)
    product(6)
    both(g_far)
    for d in (0, 1):
        g_near[d, 1 - d].start()
    bhop(3)
    piece(2)
    ag_step(1, 0)
    over_h(0)
    ag_step(1, 1)
    bhop(4)
    for d in (0, 1):
        bh[1, d].start()
    multiply([(z, w0[...])], True)

    for i in range(2, HALF):
        rs_step(i)
        if i == 2:
            for d in (0, 1):
                g_far[d].wait_recv()
                to = around(h, sign(d), NH)
                pb[to, groups[d]] = pb[to, groups[d]] + far_l[d]
                g_near[d, d].start()
        for r in (0, 1):
            ag_step(i, r)
        if i <= 3:
            bhop(i + 3)
        if i >= 3:
            rhop(i - 2)
        if i == 2:
            over_h(1)
            for d in (0, 1):
                bf[0, d].wait_recv()
            second(z)
            pair(1)
            pair(2)
            for d in (0, 1):
                for g in (0, 1):
                    g_near[d, g].wait_recv()
            q[...] = pb[h] + near_l[0] + near_l[1]
            rhop(0)
        if i == 3:
            for d in (0, 1):
                bh[2, d].start()
                bf[1, d].wait_recv()
            seconds(1, 2)
            pair(3)
        if i == 4:
            over_h(2)
            seconds(3, 3)
            pair(4)
        if i == 5:
            for d in (0, 1):
                bf[2, d].wait_recv()
            seconds(4, 4)
            pair(5)

    for half in (0, 1):
        at = pl.ds(half * 64, 64)
        for d in (0, 1):
            rsa[d, HALF - 1, half].wait_recv()
        total[at, :] = pa[HALF, at, :] + rs[0, HALF - 1, at, :] + rs[1, HALF - 1, at, :]

    def part_of(by, g):
        return pl.ds(pl.multiple_of(around(h, by, NH) * ROWS + g * 16, 16), 16)

    t_far = {d: copy(total.at[part_of(2, d)], tg.at[d], hto(sign(d)), T_SENT) for d in (0, 1)}
    t_near = {}
    for d in (0, 1):
        for g in (0, 1):
            t_near[d, g] = copy(
                total.at[part_of(sign(d), g)], ga.at[d, pl.ds(g * 16, 16)], hto(sign(d)), T_SENT
            )
    both(t_far)
    for d in (0, 1):
        t_near[d, 1 - d].start()

    for r in (0, 1):
        ag_step(HALF, r)
    far = zz_at(HALF)
    multiply([(far, tile_of(far, place(0, HALF)))])

    def block(by):
        return pl.ds(pl.multiple_of(around(x, by, NX) * 64, 64), 64)

    sides = (pl.ds(0, 256), pl.ds(256, 256))
    x_far = {d: copy(pout.at[block(2), sides[d]], tx.at[d], xto(sign(d)), X_SENT) for d in (0, 1)}
    x_near = {}
    for d in (0, 1):
        for g in (0, 1):
            x_near[d, g] = copy(
                pout.at[block(sign(d)), sides[g]], xl.at[d, :, sides[g]], xto(sign(d)), X_SENT
            )
    for d in (0, 1):
        x_far[d].start()
    for d in (0, 1):
        x_near[d, 1 - d].start()

    rhop(4)
    seconds(5, 5)
    second(far)
    for d in (0, 1):
        t_far[d].wait_recv()
        total[part_of(sign(d), d), :] = total[part_of(sign(d), d), :] + tg[d]
        t_near[d, d].start()
    for d in (0, 1):
        x_far[d].wait_recv()
        pout[block(sign(d)), sides[d]] = pout[block(sign(d)), sides[d]] + tx[d]
        x_near[d, d].start()
    rhop(5)

    def taken(ref, sem):
        pltpu.make_async_copy(ref, ref, sem).wait()

    taken(yland, y_r.at[0])

    def finish(zz, carry):
        at = lanes_of(zz)
        ig_ref[:, at] = pin[zz, l, c] + cland[zz, l] + yland[zz]
        return carry

    lax.fori_loop(0, NZ, finish, 0)
    stores = [
        pltpu.make_async_copy(a, b, o_sem.at[n])
        for n, (a, b) in enumerate(
            ((ig_ref, ig_hbm), (out_ref, out_hbm), (nw_ref, nw_hbm), (nm_ref, nm_hbm), (ns_ref, ns_hbm))
        )
    ]
    stores[0].start()
    for load in loads[3:]:
        load.wait()

    def adamw(cols, summed):
        gradient = summed * (1.0 / math.sqrt(NZ * NH * 256))
        new_mean = 0.9 * mm_v[:, cols] + 0.1 * gradient
        new_square = 0.95 * ms_v[:, cols] + 0.05 * gradient * gradient
        mean_hat = new_mean / (1.0 - 0.9**STEP)
        square_hat = new_square / (1.0 - 0.95**STEP)
        weight = w_v[:, cols]
        nw_ref[:, cols] = weight - 0.02 * (mean_hat / (jnp.sqrt(square_hat) + 1e-08) + 0.1 * weight)
        nm_ref[:, cols] = new_mean
        ns_ref[:, cols] = new_square

    for d in (0, 1):
        rz[d, HALF - 1].wait_recv()
    adamw(cols_b, q[HALF] + zb[0, HALF - 1] + zb[1, HALF - 1])

    for d in (0, 1):
        for g in (0, 1):
            x_near[d, g].wait_recv()
    out_ref[...] = pout[block(0), :] + xl[0] + xl[1]
    stores[1].start()

    for d in (0, 1):
        for g in (0, 1):
            t_near[d, g].wait_recv()
    adamw(cols_a, total[rows_of(h), :] + ga[0] + ga[1])
    for store in stores[2:]:
        store.start()

    most = pl.ds(0, NZ - 1)
    for sent, ref in (
        (H_SENT, pout.at[pl.ds(0, 3 * ROWS)]),
        (A_SENT, wa.at[most]),
        (B_SENT, q.at[most]),
        (BH_SENT, pb.at[pl.ds(0, 3), most]),
        (R_SENT, pa.at[most]),
        (G_SENT, pb.at[pl.ds(0, 3)]),
        (Q_SENT, q.at[most]),
        (X_SENT, pout.at[pl.ds(0, 192)]),
        (T_SENT, total.at[pl.ds(0, 96)]),
        (C_SENT, cland),
        (Y_SENT, yland),
    ):
        taken(ref, s_sem.at[sent])
    assert len(arrivals) == ARRIVALS, len(arrivals)
    for store in stores:
        store.wait()


def write(*refs):
    srcs, dsts, held, l_sem, o_sem = refs[:5], refs[5:10], refs[10:15], refs[15], refs[16]
    loads = [pltpu.make_async_copy(a, b, l_sem.at[n]) for n, (a, b) in enumerate(zip(srcs, held))]
    stores = [pltpu.make_async_copy(a, b, o_sem.at[n]) for n, (a, b) in enumerate(zip(held, dsts))]
    for load in loads:
        load.start()
    for load, store in zip(loads, stores):
        load.wait()
        store.start()
    for store in stores:
        store.wait()


def per_device(inputs, out_grad, weight, moment_mean, moment_square):
    dma = pltpu.SemaphoreType.DMA
    shape = jax.ShapeDtypeStruct
    hbm = pl.BlockSpec(memory_space=pl.ANY)
    small = shape((ROWS, COLS), F32)
    results = (shape((64, COLS), F32), shape((64, 1536), F32), small, small, small)

    def f32(*dims):
        return pltpu.VMEM(dims, F32)

    staged = [f32(*result.shape) for result in results]

    done = pl.pallas_call(
        kernel,
        out_shape=results,
        in_specs=[hbm] * 5,
        out_specs=[hbm] * 5,
        scratch_shapes=[
            *staged,
            f32(SLAB, COLS),
            f32(NZ, SLAB, CA),
            f32(NH, 12, ROWS, CB),
            f32(NZ, SLAB, CA),
            f32(NH, NZ, ROWS, CB),
            f32(2, HALF, SLAB, CA),
            f32(2, HALF, ROWS, CB),
            f32(2, NZ, ROWS, CB),
            f32(NZ, ROWS, CB),
            f32(2, HALF, ROWS, CB),
            f32(SLAB, CA),
            f32(2, 16, CA),
            f32(2, ROWS, CA),
            f32(256, COLS),
            f32(2, 64, 256),
            f32(2, 64, COLS),
            f32(NZ, 2, 2, 64, 128),
            f32(NZ, 2, 64, 128),
            f32(NZ, 64, 128),
            f32(256, 1536), f32(256, COLS), f32(ROWS, COLS), f32(ROWS, COLS), f32(ROWS, COLS),
            pltpu.VMEM((256, 1536), BF16),
            pltpu.VMEM((256, 1536), BF16),
            pltpu.VMEM((256, 3 * COLS), BF16),
            dma((5,)), dma((5,)),
            dma((SENDS,)), dma((ARRIVALS,)),
            dma((NZ,)), dma((1,)),
        ],
        compiler_params=pltpu.CompilerParams(
            collective_id=0, has_side_effects=True, vmem_limit_bytes=67043328
        ),
        name="step",
    )(inputs, out_grad, weight, moment_mean, moment_square)
    return pl.pallas_call(
        write,
        out_shape=results,
        in_specs=[hbm] * 5,
        out_specs=[hbm] * 5,
        scratch_shapes=[*staged, dma((5,)), dma((5,))],
        compiler_params=pltpu.CompilerParams(vmem_limit_bytes=67043328),
        name="write",
    )(*done)


def solution(mesh):
    split = Mesh(mesh.devices.reshape(NZ, NH, NX, 2, 2), ("z", "h", "x", "l", "c"))
    tile = P(("x", "z", "h"), ("l", "c"))
    return jax.shard_map(
        per_device,
        mesh=split,
        in_specs=(P(("z", "h"), "x"), P(("z", "h"), ("l", "c")), tile, tile, tile),
        out_specs=(P(("z", "h", "x"), ("l", "c")), P(("z", "h", "l", "c"), "x"), tile, tile, tile),
        check_vma=False,
    )
```

```python
import math

import jax
import jax.numpy as jnp
from jax import lax
from jax.experimental import pallas as pl
from jax.experimental.pallas import tpu as pltpu
from jax.sharding import Mesh
from jax.sharding import PartitionSpec as P

STEP = 10
NZ, NH, NX = 12, 4, 4
HALF = NZ // 2
MESH = pl.DeviceIdType.MESH
ROWS = 32
SLAB = NH * ROWS
COLS = 512
CA = 384
CB = COLS - CA
ARRIVALS = 103
SENDS = 11
F32 = jnp.float32
BF16 = jnp.bfloat16


def halves(value):
    high = value.astype(BF16)
    low = (value - high.astype(F32)).astype(BF16)
    return high, low


def dot3(a, b, dims):
    (ah, al), (bh, bl) = a, b

    def one(p, q):
        return lax.dot_general(p, q, (dims, ((), ())), preferred_element_type=F32)

    return one(ah, bh) + (one(ah, bl) + one(al, bh))


def sign(d):
    return 1 - 2 * d


def place(d, i):
    return 1 + 4 * ((i - 1) // 2) + 2 * d + (i - 1) % 2


def kernel(
    in_hbm, og_hbm, w_hbm, mm_hbm, ms_hbm,
    out_hbm, ig_hbm, nw_hbm, nm_hbm, ns_hbm,
    out_ref, ig_ref, nw_ref, nm_ref, ns_ref,
    w0, wa, wb, pa, pb, rs, far_l, near_l, q, zb, total, tg, ga, pout, tx, xl, pin, cland, yland,
    in_v, og_v, w_v, mm_v, ms_v, in_hi, in_lo, og3,
    l_sem, o_sem, s_sem, r_sem, c_r, y_r,
):
    z, h, x = lax.axis_index("z"), lax.axis_index("h"), lax.axis_index("x")
    l, c = lax.axis_index("l"), lax.axis_index("c")

    def around(at, by, n):
        return lax.rem(at + by + n, n)

    def zto(by):
        return {"z": around(z, by, NZ)}

    def hto(by):
        return {"h": around(h, by, NH)}

    def xto(by):
        return {"x": around(x, by, NX)}

    def remote(src, dst, s, r, dev):
        return pltpu.make_async_remote_copy(
            src_ref=src, dst_ref=dst, send_sem=s, recv_sem=r, device_id=dev, device_id_type=MESH
        )

    arrivals = []

    def arrival():
        arrivals.append(len(arrivals))
        return arrivals[-1]

    H_SENT, A_SENT, B_SENT, BH_SENT, R_SENT, G_SENT, Q_SENT, X_SENT, T_SENT, C_SENT, Y_SENT = range(SENDS)

    def copy(src, dst, dev, sent, at=None):
        return remote(src, dst, s_sem.at[sent], r_sem.at[arrival() if at is None else at], dev)

    loads = [
        pltpu.make_async_copy(a, b, l_sem.at[n])
        for n, (a, b) in enumerate(
            ((w_hbm, w_v), (og_hbm, og_v), (in_hbm, in_v), (mm_hbm, mm_v), (ms_hbm, ms_v))
        )
    ]
    for load in loads:
        load.start()

    partners = [zto(1), zto(-1), {"c": 1 - c}, {"l": 1 - l}]
    partners += [hto(j) for j in (1, 2, 3)] + [xto(j) for j in (1, -1)]
    barrier = pltpu.get_barrier_semaphore()
    for dev in partners:
        pl.semaphore_signal(barrier, inc=1, device_id=dev, device_id_type=MESH)
    pl.semaphore_wait(barrier, len(partners))

    def zz_at(by):
        return around(z, by, NZ)

    def rows_of(hh):
        return pl.ds(pl.multiple_of(hh * ROWS, ROWS), ROWS)

    def lanes_of(zz):
        return pl.ds(pl.multiple_of(zz * SLAB, SLAB), SLAB)

    cols_a, cols_b = pl.ds(0, CA), pl.ds(CA, CB)

    own_h = {j: copy(w_hbm, w0.at[rows_of(h)], hto(j), H_SENT) for j in (1, 3, 2)}
    ag, came = {}, {}
    for d in (0, 1):
        for k in range(NH):
            at = rows_of(around(h, -k, NH))
            src = w_hbm.at[:, cols_a] if k == 0 else w0.at[at, cols_a]
            ids = arrival()
            came[d] = ids - k
            ag[d, 0, k] = copy(src, wa.at[z, at], zto(sign(d)), A_SENT, ids)
    near_half = h // 2

    def half_of(r):
        return pl.ds(pl.multiple_of((near_half if r == 0 else 1 - near_half) * 64, 64), 64)

    for i in range(1, HALF):
        for d in (0, 1):
            for r in (0, 1):
                if i < HALF - 1 or r == d:
                    here = wa.at[zz_at(-sign(d) * i), half_of(r)]
                    ag[d, i, r] = copy(here, here, zto(sign(d)), A_SENT)

    bz = {}
    for i in range(HALF):
        for d in (0, 1):
            if i < HALF - 1 or d == 0:
                src = w_hbm.at[:, cols_b] if i == 0 else wb.at[h, place(d, i)]
                bz[d, i] = copy(src, wb.at[h, place(d, i + 1)], zto(sign(d)), B_SENT)
    bh, bf = {}, {}
    for b in range(3):
        n = 4 if b < 2 else 3
        for d in (0, 1):
            at = pl.ds(1 + 4 * b, n)
            bh[b, d] = copy(wb.at[h, at], wb.at[h, at], hto(sign(d)), BH_SENT)
            at = pl.ds(1 + 4 * b + 2 * d, 2 if d == 0 else n - 2)
            back = around(h, -sign(d), NH)
            bf[b, d] = copy(wb.at[back, at], wb.at[back, at], hto(sign(d)), BH_SENT)

    def bhop(i):
        for d in (0, 1):
            if (d, i - 1) in bz:
                bz[d, i - 1].wait_recv()
                if (d, i) in bz:
                    bz[d, i].start()

    def rows_in(r):
        return half_of(1 - r)

    rsa = {}
    for i in range(HALF):
        for d in (0, 1):
            for half in (0, 1):
                if i > 0 or half == d:
                    at = rows_in(half)
                    src = pa.at[0, at] if i == 0 else rs.at[d, i - 1, at]
                    rsa[d, i, half] = copy(src, rs.at[d, i, at], zto(sign(d)), R_SENT)

    groups = (pl.ds(0, HALF), pl.ds(HALF, HALF))
    two = around(h, 2, NH)
    g_far = {d: copy(pb.at[two, groups[d]], far_l.at[d], hto(sign(d)), G_SENT) for d in (0, 1)}
    g_near = {}
    for d in (0, 1):
        to = around(h, sign(d), NH)
        for g in (0, 1):
            g_near[d, g] = copy(pb.at[to, groups[g]], near_l.at[d, groups[g]], hto(sign(d)), G_SENT)
    rz = {}
    for j in range(HALF):
        for d in (0, 1):
            if j >= d:
                src = q.at[0 if d == 0 else NZ - 1] if j == d else zb.at[d, j - 1]
                rz[d, j] = copy(src, zb.at[d, j], zto(sign(d)), Q_SENT)

    def rhop(j):
        for d in (0, 1):
            if j < d:
                continue
            if j > d:
                rz[d, j - 1].wait_recv()
                zb[d, j - 1] = zb[d, j - 1] + q[j if d == 0 else NZ - j]
            rz[d, j].start()

    for d in (0, 1):
        ag[d, 0, 0].start()
        bz[d, 0].start()
    for j in (1, 3, 2):
        own_h[j].start()

    for load in loads[:3]:
        load.wait()
    w0[rows_of(h), :] = w_v[...]
    high, low = halves(og_v[...])
    og3[...] = jnp.concatenate([high, high, low], axis=1)
    in_hi[...], in_lo[...] = halves(in_v[...])

    def og():
        return og3[:, :COLS], og3[:, 2 * COLS :]

    def product(s):
        at = lanes_of(zz_at(HALF - s))
        part = dot3((in_hi[:, at], in_lo[:, at]), og(), ((0,), (0,)))
        pa[s] = part[:, :CA]
        pb[:, s] = part[:, CA:].reshape(NH, ROWS, CB)

    def c_copy(zz):
        return remote(pin.at[zz, :, 1 - c], cland.at[zz], s_sem.at[C_SENT], c_r.at[zz], {"c": 1 - c})

    def y_copy(zz):
        return remote(pin.at[zz, 1 - l, c], yland.at[zz], s_sem.at[Y_SENT], y_r.at[0], {"l": 1 - l})

    def multiply(parts, start=False):
        across, down, left = [], [], []
        for zz, tile in parts:
            high, low = halves(tile)
            at = lanes_of(zz)
            across.append(jnp.concatenate([high, low, high], axis=1))
            down += [high, low, high]
            left += [in_hi[:, at], in_hi[:, at], in_lo[:, at]]
        part = lax.dot_general(
            og3[...], jnp.concatenate(across, axis=0), (((1,), (1,)), ((), ())), preferred_element_type=F32
        )
        for n, (zz, _) in enumerate(parts):
            pin[zz] = part[:, n * SLAB : (n + 1) * SLAB].reshape(2, 2, 64, SLAB)
            c_copy(zz).start()
        out = jnp.dot(
            jnp.concatenate(left, axis=1), jnp.concatenate(down, axis=0), preferred_element_type=F32
        )
        pout[...] = out if start else pout[...] + out

    def tile_of(zz, at):
        return jnp.concatenate([wa[zz], wb[:, at].reshape(SLAB, CB)], axis=1)

    def pair(i):
        both = [zz_at(-sign(d) * i) for d in (0, 1)]
        multiply([(zz, tile_of(zz, place(d, i))) for d, zz in enumerate(both)])

    def second(zz):
        c_copy(zz).wait_recv()
        pin[zz, 1 - l, c] = pin[zz, 1 - l, c] + cland[zz, 1 - l]
        y_copy(zz).start()

    def seconds(first, last):
        def each(n, carry):
            second(zz_at((2 * (n % 2) - 1) * (first + n // 2)))
            return carry

        lax.fori_loop(0, 2 * (last - first + 1), each, 0)

    def ag_step(i, r):
        for d in (0, 1):
            if i == 1:
                odd = h % 2
                for k in (0, 3 - 2 * odd) if r == 0 else (1 + 2 * odd, 2):
                    piece = wa.at[z, rows_of(0)]
                    remote(piece, piece, s_sem.at[A_SENT], r_sem.at[came[d] + k], zto(1)).wait_recv()
            elif (d, i - 1, r) in ag:
                ag[d, i - 1, r].wait_recv()
            if (d, i, r) in ag and i > 0:
                ag[d, i, r].start()

    def rs_step(i, half):
        for d in (0, 1):
            at = rows_in(half)
            mine = pa[i if d == 0 else NZ - i, at, :]
            if (d, i - 1, half) in rsa:
                rsa[d, i - 1, half].wait_recv()
                rs[d, i - 1, at, :] = rs[d, i - 1, at, :] + mine
            else:
                rs[d, i - 1, at, :] = mine
            rsa[d, i, half].start()

    def both(copies):
        for d in (0, 1):
            copies[d].start()

    def over_h(b):
        for d in (0, 1):
            bh[b, d].wait_recv()
            bf[b, d].start()

    def piece(k):
        own_h[k].wait_recv()
        for d in (0, 1):
            ag[d, 0, k].start()

    product(0)
    rsa[0, 0, 0].start()
    rsa[1, 0, 1].start()
    for n in range(1, HALF):
        product(n)
        product(NZ - n)
    product(HALF)
    both(g_far)
    for d in (0, 1):
        g_near[d, 1 - d].start()
    bhop(1)
    piece(1)
    bhop(2)
    piece(3)
    rs_step(1, 0)
    rs_step(1, 1)
    bhop(3)
    piece(2)
    ag_step(1, 0)
    for d in (0, 1):
        g_far[d].wait_recv()
        to = around(h, sign(d), NH)
        pb[to, groups[d]] = pb[to, groups[d]] + far_l[d]
        g_near[d, d].start()
    ag_step(1, 1)
    bhop(4)
    for d in (0, 1):
        bh[0, d].start()
    multiply([(z, w0[...])], True)

    for i in range(2, HALF):
        turns = {2: "rraa", 3: "rara", 4: "arar", 5: "aarr"}[i]
        for n, turn in enumerate(turns):
            (rs_step if turn == "r" else ag_step)(i, turns[:n].count(turn))
            if n == 1 and i == 4:
                for d in (0, 1):
                    bf[0, d].wait_recv()
                pair(1)
                pair(2)
            if n == 1 and i == 5:
                seconds(1, 4)
        if i <= 3:
            bhop(i + 3)
            for d in (0, 1):
                bh[i - 1, d].start()
        if i == 2:
            for d in (0, 1):
                for g in (0, 1):
                    g_near[d, g].wait_recv()
            q[...] = pb[h] + near_l[0] + near_l[1]
        rhop(i - 2)
        if i == 2:
            second(z)
        if i == 3:
            over_h(0)
            over_h(1)
        if i == 4:
            over_h(2)
            for d in (0, 1):
                bf[1, d].wait_recv()
            pair(3)
            pair(4)
        if i == 5:
            for d in (0, 1):
                bf[2, d].wait_recv()
            pair(5)

    for r in (0, 1):
        ag_step(HALF, r)
    far = zz_at(HALF)
    multiply([(far, tile_of(far, place(0, HALF)))])

    def block(by):
        return pl.ds(pl.multiple_of(around(x, by, NX) * 64, 64), 64)

    sides = (pl.ds(0, 256), pl.ds(256, 256))
    x_far = {d: copy(pout.at[block(2), sides[d]], tx.at[d], xto(sign(d)), X_SENT) for d in (0, 1)}
    x_near = {}
    for d in (0, 1):
        for g in (0, 1):
            x_near[d, g] = copy(
                pout.at[block(sign(d)), sides[g]], xl.at[d, :, sides[g]], xto(sign(d)), X_SENT
            )
    for d in (0, 1):
        x_far[d].start()
    for d in (0, 1):
        x_near[d, 1 - d].start()

    def add_up(half):
        at = rows_in(half)
        for d in (0, 1):
            rsa[d, HALF - 1, half].wait_recv()
        total[at, :] = pa[HALF, at, :] + rs[0, HALF - 1, at, :] + rs[1, HALF - 1, at, :]

    def part_of(by, g):
        return pl.ds(pl.multiple_of(around(h, by, NH) * ROWS + g * 16, 16), 16)

    t_far = {d: copy(total.at[part_of(2, d)], tg.at[d], hto(sign(d)), T_SENT) for d in (0, 1)}
    t_near = {}
    for d in (0, 1):
        for g in (0, 1):
            t_near[d, g] = copy(
                total.at[part_of(sign(d), g)], ga.at[d, pl.ds(g * 16, 16)], hto(sign(d)), T_SENT
            )
    add_up(0)
    both(t_far)
    add_up(1)
    for d in (0, 1):
        t_near[d, 1 - d].start()

    rhop(4)
    seconds(5, 5)
    second(far)
    for d in (0, 1):
        x_far[d].wait_recv()
        pout[block(sign(d)), sides[d]] = pout[block(sign(d)), sides[d]] + tx[d]
        x_near[d, d].start()
    rhop(5)
    for d in (0, 1):
        t_far[d].wait_recv()
        total[part_of(sign(d), d), :] = total[part_of(sign(d), d), :] + tg[d]
        t_near[d, d].start()

    def taken(ref, sem):
        pltpu.make_async_copy(ref, ref, sem).wait()

    taken(yland, y_r.at[0])

    def finish(zz, carry):
        at = lanes_of(zz)
        ig_ref[:, at] = pin[zz, l, c] + cland[zz, l] + yland[zz]
        return carry

    lax.fori_loop(0, NZ, finish, 0)
    stores = [
        pltpu.make_async_copy(a, b, o_sem.at[n])
        for n, (a, b) in enumerate(
            ((ig_ref, ig_hbm), (out_ref, out_hbm), (nw_ref, nw_hbm), (nm_ref, nm_hbm), (ns_ref, ns_hbm))
        )
    ]
    stores[0].start()
    for load in loads[3:]:
        load.wait()

    def adamw(cols, summed):
        gradient = summed * (1.0 / math.sqrt(NZ * NH * 256))
        new_mean = 0.9 * mm_v[:, cols] + 0.1 * gradient
        new_square = 0.95 * ms_v[:, cols] + 0.05 * gradient * gradient
        mean_hat = new_mean / (1.0 - 0.9**STEP)
        square_hat = new_square / (1.0 - 0.95**STEP)
        weight = w_v[:, cols]
        nw_ref[:, cols] = weight - 0.02 * (mean_hat / (jnp.sqrt(square_hat) + 1e-08) + 0.1 * weight)
        nm_ref[:, cols] = new_mean
        ns_ref[:, cols] = new_square

    for d in (0, 1):
        rz[d, HALF - 1].wait_recv()
    adamw(cols_b, q[HALF] + zb[0, HALF - 1] + zb[1, HALF - 1])

    for d in (0, 1):
        for g in (0, 1):
            x_near[d, g].wait_recv()
    out_ref[...] = pout[block(0), :] + xl[0] + xl[1]
    stores[1].start()

    for d in (0, 1):
        for g in (0, 1):
            t_near[d, g].wait_recv()
    adamw(cols_a, total[rows_of(h), :] + ga[0] + ga[1])
    for store in stores[2:]:
        store.start()

    most = pl.ds(0, NZ - 1)
    for sent, ref in (
        (H_SENT, pout.at[pl.ds(0, 3 * ROWS)]),
        (A_SENT, wa.at[most]),
        (B_SENT, q.at[most]),
        (BH_SENT, pb.at[pl.ds(0, 3), most]),
        (R_SENT, pa.at[most]),
        (G_SENT, pb.at[pl.ds(0, 3)]),
        (Q_SENT, q.at[most]),
        (X_SENT, pout.at[pl.ds(0, 192)]),
        (T_SENT, total.at[pl.ds(0, 96)]),
        (C_SENT, cland),
        (Y_SENT, yland),
    ):
        taken(ref, s_sem.at[sent])
    assert len(arrivals) == ARRIVALS, len(arrivals)
    for store in stores:
        store.wait()


def write(*refs):
    srcs, dsts, held, l_sem, o_sem = refs[:5], refs[5:10], refs[10:15], refs[15], refs[16]
    loads = [pltpu.make_async_copy(a, b, l_sem.at[n]) for n, (a, b) in enumerate(zip(srcs, held))]
    stores = [pltpu.make_async_copy(a, b, o_sem.at[n]) for n, (a, b) in enumerate(zip(held, dsts))]
    for load in loads:
        load.start()
    for load, store in zip(loads, stores):
        load.wait()
        store.start()
    for store in stores:
        store.wait()


def per_device(inputs, out_grad, weight, moment_mean, moment_square):
    dma = pltpu.SemaphoreType.DMA
    shape = jax.ShapeDtypeStruct
    hbm = pl.BlockSpec(memory_space=pl.ANY)
    small = shape((ROWS, COLS), F32)
    results = (shape((64, COLS), F32), shape((64, 1536), F32), small, small, small)

    def f32(*dims):
        return pltpu.VMEM(dims, F32)

    staged = [f32(*result.shape) for result in results]

    done = pl.pallas_call(
        kernel,
        out_shape=results,
        in_specs=[hbm] * 5,
        out_specs=[hbm] * 5,
        scratch_shapes=[
            *staged,
            f32(SLAB, COLS),
            f32(NZ, SLAB, CA),
            f32(NH, 12, ROWS, CB),
            f32(NZ, SLAB, CA),
            f32(NH, NZ, ROWS, CB),
            f32(2, HALF, SLAB, CA),
            f32(2, HALF, ROWS, CB),
            f32(2, NZ, ROWS, CB),
            f32(NZ, ROWS, CB),
            f32(2, HALF, ROWS, CB),
            f32(SLAB, CA),
            f32(2, 16, CA),
            f32(2, ROWS, CA),
            f32(256, COLS),
            f32(2, 64, 256),
            f32(2, 64, COLS),
            f32(NZ, 2, 2, 64, 128),
            f32(NZ, 2, 64, 128),
            f32(NZ, 64, 128),
            f32(256, 1536), f32(256, COLS), f32(ROWS, COLS), f32(ROWS, COLS), f32(ROWS, COLS),
            pltpu.VMEM((256, 1536), BF16),
            pltpu.VMEM((256, 1536), BF16),
            pltpu.VMEM((256, 3 * COLS), BF16),
            dma((5,)), dma((5,)),
            dma((SENDS,)), dma((ARRIVALS,)),
            dma((NZ,)), dma((1,)),
        ],
        compiler_params=pltpu.CompilerParams(
            collective_id=0, has_side_effects=True, vmem_limit_bytes=67043328
        ),
        name="step",
    )(inputs, out_grad, weight, moment_mean, moment_square)
    return pl.pallas_call(
        write,
        out_shape=results,
        in_specs=[hbm] * 5,
        out_specs=[hbm] * 5,
        scratch_shapes=[*staged, dma((5,)), dma((5,))],
        compiler_params=pltpu.CompilerParams(vmem_limit_bytes=67043328),
        name="write",
    )(*done)


def solution(mesh):
    split = Mesh(mesh.devices.reshape(NZ, NH, NX, 2, 2), ("z", "h", "x", "l", "c"))
    tile = P(("x", "z", "h"), ("l", "c"))
    return jax.shard_map(
        per_device,
        mesh=split,
        in_specs=(P(("z", "h"), "x"), P(("z", "h"), ("l", "c")), tile, tile, tile),
        out_specs=(P(("z", "h", "x"), ("l", "c")), P(("z", "h", "l", "c"), "x"), tile, tile, tile),
        check_vma=False,
    )
```

```python
import math

import jax
import jax.numpy as jnp
from jax import lax
from jax.experimental import pallas as pl
from jax.experimental.pallas import tpu as pltpu
from jax.sharding import Mesh
from jax.sharding import PartitionSpec as P

STEP = 10
NZ, NH, NX = 12, 4, 4
HALF = NZ // 2
MESH = pl.DeviceIdType.MESH
ROWS = 32
SLAB = NH * ROWS
COLS = 512
CA = 384
CB = COLS - CA
ARRIVALS = 103
SENDS = 11
F32 = jnp.float32
BF16 = jnp.bfloat16


def halves(value):
    high = value.astype(BF16)
    low = (value - high.astype(F32)).astype(BF16)
    return high, low


def dot3(a, b, dims):
    (ah, al), (bh, bl) = a, b

    def one(p, q):
        return lax.dot_general(p, q, (dims, ((), ())), preferred_element_type=F32)

    return one(ah, bh) + (one(ah, bl) + one(al, bh))


def sign(d):
    return 1 - 2 * d


def place(d, i):
    return 1 + 4 * ((i - 1) // 2) + 2 * d + (i - 1) % 2


def kernel(
    in_hbm, og_hbm, w_hbm, mm_hbm, ms_hbm,
    out_ref, ig_ref, nw_ref, nm_ref, ns_ref,
    w0, wa, wb, pa, pb, rs, far_l, near_l, q, zb, total, tg, ga, pout, tx, xl, pin, cland, yland,
    in_v, og_v, w_v, mm_v, ms_v, in_hi, in_lo, og3,
    l_sem, s_sem, r_sem, c_r, y_r,
):
    z, h, x = lax.axis_index("z"), lax.axis_index("h"), lax.axis_index("x")
    l, c = lax.axis_index("l"), lax.axis_index("c")

    def around(at, by, n):
        return lax.rem(at + by + n, n)

    def zto(by):
        return {"z": around(z, by, NZ)}

    def hto(by):
        return {"h": around(h, by, NH)}

    def xto(by):
        return {"x": around(x, by, NX)}

    def remote(src, dst, s, r, dev):
        return pltpu.make_async_remote_copy(
            src_ref=src, dst_ref=dst, send_sem=s, recv_sem=r, device_id=dev, device_id_type=MESH
        )

    arrivals = []

    def arrival():
        arrivals.append(len(arrivals))
        return arrivals[-1]

    H_SENT, A_SENT, B_SENT, BH_SENT, R_SENT, G_SENT, Q_SENT, X_SENT, T_SENT, C_SENT, Y_SENT = range(SENDS)

    def copy(src, dst, dev, sent, at=None):
        return remote(src, dst, s_sem.at[sent], r_sem.at[arrival() if at is None else at], dev)

    loads = [
        pltpu.make_async_copy(a, b, l_sem.at[n])
        for n, (a, b) in enumerate(
            ((w_hbm, w_v), (og_hbm, og_v), (in_hbm, in_v), (mm_hbm, mm_v), (ms_hbm, ms_v))
        )
    ]
    for load in loads:
        load.start()

    partners = [zto(1), zto(-1), {"c": 1 - c}, {"l": 1 - l}]
    partners += [hto(j) for j in (1, 2, 3)] + [xto(j) for j in (1, -1)]
    barrier = pltpu.get_barrier_semaphore()
    for dev in partners:
        pl.semaphore_signal(barrier, inc=1, device_id=dev, device_id_type=MESH)
    pl.semaphore_wait(barrier, len(partners))

    def zz_at(by):
        return around(z, by, NZ)

    def rows_of(hh):
        return pl.ds(pl.multiple_of(hh * ROWS, ROWS), ROWS)

    def lanes_of(zz):
        return pl.ds(pl.multiple_of(zz * SLAB, SLAB), SLAB)

    cols_a, cols_b = pl.ds(0, CA), pl.ds(CA, CB)

    own_h = {j: copy(w_hbm, w0.at[rows_of(h)], hto(j), H_SENT) for j in (1, 3, 2)}
    ag, came = {}, {}
    for d in (0, 1):
        for k in range(NH):
            at = rows_of(around(h, -k, NH))
            src = w_hbm.at[:, cols_a] if k == 0 else w0.at[at, cols_a]
            ids = arrival()
            came[d] = ids - k
            ag[d, 0, k] = copy(src, wa.at[z, at], zto(sign(d)), A_SENT, ids)
    near_half = h // 2

    def half_of(r):
        return pl.ds(pl.multiple_of((near_half if r == 0 else 1 - near_half) * 64, 64), 64)

    for i in range(1, HALF):
        for d in (0, 1):
            for r in (0, 1):
                if i < HALF - 1 or r == d:
                    here = wa.at[zz_at(-sign(d) * i), half_of(r)]
                    ag[d, i, r] = copy(here, here, zto(sign(d)), A_SENT)

    bz = {}
    for i in range(HALF):
        for d in (0, 1):
            if i < HALF - 1 or d == 0:
                src = w_hbm.at[:, cols_b] if i == 0 else wb.at[h, place(d, i)]
                bz[d, i] = copy(src, wb.at[h, place(d, i + 1)], zto(sign(d)), B_SENT)
    bh, bf = {}, {}
    for b in range(3):
        n = 4 if b < 2 else 3
        for d in (0, 1):
            at = pl.ds(1 + 4 * b, n)
            bh[b, d] = copy(wb.at[h, at], wb.at[h, at], hto(sign(d)), BH_SENT)
            at = pl.ds(1 + 4 * b + 2 * d, 2 if d == 0 else n - 2)
            back = around(h, -sign(d), NH)
            bf[b, d] = copy(wb.at[back, at], wb.at[back, at], hto(sign(d)), BH_SENT)

    def bhop(i):
        for d in (0, 1):
            if (d, i - 1) in bz:
                bz[d, i - 1].wait_recv()
                if (d, i) in bz:
                    bz[d, i].start()

    def rows_in(r):
        return half_of(1 - r)

    rsa = {}
    for i in range(HALF):
        for d in (0, 1):
            for half in (0, 1):
                if i > 0 or half == d:
                    at = rows_in(half)
                    src = pa.at[0, at] if i == 0 else rs.at[d, i - 1, at]
                    rsa[d, i, half] = copy(src, rs.at[d, i, at], zto(sign(d)), R_SENT)

    groups = (pl.ds(0, HALF), pl.ds(HALF, HALF))
    two = around(h, 2, NH)
    g_far = {d: copy(pb.at[two, groups[d]], far_l.at[d], hto(sign(d)), G_SENT) for d in (0, 1)}
    g_near = {}
    for d in (0, 1):
        to = around(h, sign(d), NH)
        for g in (0, 1):
            g_near[d, g] = copy(pb.at[to, groups[g]], near_l.at[d, groups[g]], hto(sign(d)), G_SENT)
    rz = {}
    for j in range(HALF):
        for d in (0, 1):
            if j >= d:
                src = q.at[0 if d == 0 else NZ - 1] if j == d else zb.at[d, j - 1]
                rz[d, j] = copy(src, zb.at[d, j], zto(sign(d)), Q_SENT)

    def rhop(j):
        for d in (0, 1):
            if j < d:
                continue
            if j > d:
                rz[d, j - 1].wait_recv()
                zb[d, j - 1] = zb[d, j - 1] + q[j if d == 0 else NZ - j]
            rz[d, j].start()

    for d in (0, 1):
        ag[d, 0, 0].start()
        bz[d, 0].start()
    for j in (1, 3, 2):
        own_h[j].start()

    for load in loads[:3]:
        load.wait()
    w0[rows_of(h), :] = w_v[...]
    high, low = halves(og_v[...])
    og3[...] = jnp.concatenate([high, high, low], axis=1)
    in_hi[...], in_lo[...] = halves(in_v[...])

    def og():
        return og3[:, :COLS], og3[:, 2 * COLS :]

    def product(s):
        at = lanes_of(zz_at(HALF - s))
        part = dot3((in_hi[:, at], in_lo[:, at]), og(), ((0,), (0,)))
        pa[s] = part[:, :CA]
        pb[:, s] = part[:, CA:].reshape(NH, ROWS, CB)

    def c_copy(zz):
        return remote(pin.at[zz, :, 1 - c], cland.at[zz], s_sem.at[C_SENT], c_r.at[zz], {"c": 1 - c})

    def y_copy(zz):
        return remote(pin.at[zz, 1 - l, c], yland.at[zz], s_sem.at[Y_SENT], y_r.at[0], {"l": 1 - l})

    def multiply(parts, start=False):
        across, down, left = [], [], []
        for zz, tile in parts:
            high, low = halves(tile)
            at = lanes_of(zz)
            across.append(jnp.concatenate([high, low, high], axis=1))
            down += [high, low, high]
            left += [in_hi[:, at], in_hi[:, at], in_lo[:, at]]
        part = lax.dot_general(
            og3[...], jnp.concatenate(across, axis=0), (((1,), (1,)), ((), ())), preferred_element_type=F32
        )
        for n, (zz, _) in enumerate(parts):
            pin[zz] = part[:, n * SLAB : (n + 1) * SLAB].reshape(2, 2, 64, SLAB)
            c_copy(zz).start()
        out = jnp.dot(
            jnp.concatenate(left, axis=1), jnp.concatenate(down, axis=0), preferred_element_type=F32
        )
        pout[...] = out if start else pout[...] + out

    def tile_of(zz, at):
        return jnp.concatenate([wa[zz], wb[:, at].reshape(SLAB, CB)], axis=1)

    def pair(i):
        both = [zz_at(-sign(d) * i) for d in (0, 1)]
        multiply([(zz, tile_of(zz, place(d, i))) for d, zz in enumerate(both)])

    def second(zz):
        c_copy(zz).wait_recv()
        pin[zz, 1 - l, c] = pin[zz, 1 - l, c] + cland[zz, 1 - l]
        y_copy(zz).start()

    def seconds(first, last):
        def each(n, carry):
            second(zz_at((2 * (n % 2) - 1) * (first + n // 2)))
            return carry

        lax.fori_loop(0, 2 * (last - first + 1), each, 0)

    def ag_step(i, r):
        for d in (0, 1):
            if i == 1:
                odd = h % 2
                for k in (0, 3 - 2 * odd) if r == 0 else (1 + 2 * odd, 2):
                    piece = wa.at[z, rows_of(0)]
                    remote(piece, piece, s_sem.at[A_SENT], r_sem.at[came[d] + k], zto(1)).wait_recv()
            elif (d, i - 1, r) in ag:
                ag[d, i - 1, r].wait_recv()
            if (d, i, r) in ag and i > 0:
                ag[d, i, r].start()

    def rs_step(i, half):
        for d in (0, 1):
            at = rows_in(half)
            mine = pa[i if d == 0 else NZ - i, at, :]
            if (d, i - 1, half) in rsa:
                rsa[d, i - 1, half].wait_recv()
                rs[d, i - 1, at, :] = rs[d, i - 1, at, :] + mine
            else:
                rs[d, i - 1, at, :] = mine
            rsa[d, i, half].start()

    def both(copies):
        for d in (0, 1):
            copies[d].start()

    def over_h(b):
        for d in (0, 1):
            bh[b, d].wait_recv()
            bf[b, d].start()

    def piece(k):
        own_h[k].wait_recv()
        for d in (0, 1):
            ag[d, 0, k].start()

    product(0)
    rsa[0, 0, 0].start()
    rsa[1, 0, 1].start()
    bhop(1)
    product(1)
    product(NZ - 1)
    piece(1)
    product(2)
    product(NZ - 2)
    bhop(2)
    for d in (0, 1):
        bh[0, d].start()
    piece(3)
    product(3)
    product(NZ - 3)
    rs_step(1, 0)
    rs_step(1, 1)
    product(4)
    product(NZ - 4)
    product(5)
    product(NZ - 5)
    product(6)
    both(g_far)
    for d in (0, 1):
        g_near[d, 1 - d].start()
    bhop(3)
    piece(2)
    ag_step(1, 0)
    over_h(0)
    ag_step(1, 1)
    bhop(4)
    for d in (0, 1):
        bh[1, d].start()
    multiply([(z, w0[...])], True)

    for i in range(2, HALF):
        turns = {2: "rr", 3: "rara", 4: "arar", 5: "aarr"}[i]
        for n, turn in enumerate(turns):
            (rs_step if turn == "r" else ag_step)(i, turns[:n].count(turn))
        if i == 2:
            for d in (0, 1):
                g_far[d].wait_recv()
                to = around(h, sign(d), NH)
                pb[to, groups[d]] = pb[to, groups[d]] + far_l[d]
                g_near[d, d].start()
            ag_step(i, 0)
            ag_step(i, 1)
        if i <= 3:
            bhop(i + 3)
        if i >= 3:
            rhop(i - 2)
        if i == 2:
            over_h(1)
            for d in (0, 1):
                bf[0, d].wait_recv()
            second(z)
            pair(1)
            pair(2)
            for d in (0, 1):
                for g in (0, 1):
                    g_near[d, g].wait_recv()
            q[...] = pb[h] + near_l[0] + near_l[1]
            rhop(0)
        if i == 3:
            for d in (0, 1):
                bh[2, d].start()
                bf[1, d].wait_recv()
            seconds(1, 2)
            pair(3)
        if i == 4:
            over_h(2)
            seconds(3, 3)
            pair(4)
        if i == 5:
            for d in (0, 1):
                bf[2, d].wait_recv()
            seconds(4, 4)
            pair(5)

    for r in (0, 1):
        ag_step(HALF, r)
    far = zz_at(HALF)
    multiply([(far, tile_of(far, place(0, HALF)))])

    def block(by):
        return pl.ds(pl.multiple_of(around(x, by, NX) * 64, 64), 64)

    sides = (pl.ds(0, 256), pl.ds(256, 256))
    x_far = {d: copy(pout.at[block(2), sides[d]], tx.at[d], xto(sign(d)), X_SENT) for d in (0, 1)}
    x_near = {}
    for d in (0, 1):
        for g in (0, 1):
            x_near[d, g] = copy(
                pout.at[block(sign(d)), sides[g]], xl.at[d, :, sides[g]], xto(sign(d)), X_SENT
            )
    for d in (0, 1):
        x_far[d].start()
    for d in (0, 1):
        x_near[d, 1 - d].start()

    def add_up(half):
        at = rows_in(half)
        for d in (0, 1):
            rsa[d, HALF - 1, half].wait_recv()
        total[at, :] = pa[HALF, at, :] + rs[0, HALF - 1, at, :] + rs[1, HALF - 1, at, :]

    def part_of(by, g):
        return pl.ds(pl.multiple_of(around(h, by, NH) * ROWS + g * 16, 16), 16)

    t_far = {d: copy(total.at[part_of(2, d)], tg.at[d], hto(sign(d)), T_SENT) for d in (0, 1)}
    t_near = {}
    for d in (0, 1):
        for g in (0, 1):
            t_near[d, g] = copy(
                total.at[part_of(sign(d), g)], ga.at[d, pl.ds(g * 16, 16)], hto(sign(d)), T_SENT
            )
    add_up(0)
    both(t_far)
    add_up(1)
    for d in (0, 1):
        t_near[d, 1 - d].start()

    rhop(4)
    seconds(5, 5)
    second(far)
    for d in (0, 1):
        x_far[d].wait_recv()
        pout[block(sign(d)), sides[d]] = pout[block(sign(d)), sides[d]] + tx[d]
        x_near[d, d].start()
    for d in (0, 1):
        t_far[d].wait_recv()
        total[part_of(sign(d), d), :] = total[part_of(sign(d), d), :] + tg[d]
        t_near[d, d].start()
    rhop(5)

    def taken(ref, sem):
        pltpu.make_async_copy(ref, ref, sem).wait()

    taken(yland, y_r.at[0])

    def finish(zz, carry):
        at = lanes_of(zz)
        ig_ref[:, at] = pin[zz, l, c] + cland[zz, l] + yland[zz]
        return carry

    lax.fori_loop(0, NZ, finish, 0)
    for load in loads[3:]:
        load.wait()

    def adamw(cols, summed):
        gradient = summed * (1.0 / math.sqrt(NZ * NH * 256))
        new_mean = 0.9 * mm_v[:, cols] + 0.1 * gradient
        new_square = 0.95 * ms_v[:, cols] + 0.05 * gradient * gradient
        mean_hat = new_mean / (1.0 - 0.9**STEP)
        square_hat = new_square / (1.0 - 0.95**STEP)
        weight = w_v[:, cols]
        nw_ref[:, cols] = weight - 0.02 * (mean_hat / (jnp.sqrt(square_hat) + 1e-08) + 0.1 * weight)
        nm_ref[:, cols] = new_mean
        ns_ref[:, cols] = new_square

    for d in (0, 1):
        rz[d, HALF - 1].wait_recv()
    adamw(cols_b, q[HALF] + zb[0, HALF - 1] + zb[1, HALF - 1])

    for d in (0, 1):
        for g in (0, 1):
            x_near[d, g].wait_recv()
    out_ref[...] = pout[block(0), :] + xl[0] + xl[1]

    for d in (0, 1):
        for g in (0, 1):
            t_near[d, g].wait_recv()
    adamw(cols_a, total[rows_of(h), :] + ga[0] + ga[1])

    most = pl.ds(0, NZ - 1)
    for sent, ref in (
        (H_SENT, pout.at[pl.ds(0, 3 * ROWS)]),
        (A_SENT, wa.at[most]),
        (B_SENT, q.at[most]),
        (BH_SENT, pb.at[pl.ds(0, 3), most]),
        (R_SENT, pa.at[most]),
        (G_SENT, pb.at[pl.ds(0, 3)]),
        (Q_SENT, q.at[most]),
        (X_SENT, pout.at[pl.ds(0, 192)]),
        (T_SENT, total.at[pl.ds(0, 96)]),
        (C_SENT, cland),
        (Y_SENT, yland),
    ):
        taken(ref, s_sem.at[sent])
    assert len(arrivals) == ARRIVALS, len(arrivals)


def write(*refs):
    held, dsts, o_sem = refs[:5], refs[5:10], refs[10]
    stores = [pltpu.make_async_copy(a, b, o_sem.at[n]) for n, (a, b) in enumerate(zip(held, dsts))]
    for store in stores:
        store.start()
    for store in stores:
        store.wait()


def per_device(inputs, out_grad, weight, moment_mean, moment_square):
    dma = pltpu.SemaphoreType.DMA
    shape = jax.ShapeDtypeStruct
    hbm = pl.BlockSpec(memory_space=pl.ANY)
    small = shape((ROWS, COLS), F32)
    results = (shape((64, COLS), F32), shape((64, 1536), F32), small, small, small)

    def f32(*dims):
        return pltpu.VMEM(dims, F32)

    vmem = pl.BlockSpec(memory_space=pltpu.VMEM)

    done = pl.pallas_call(
        kernel,
        out_shape=results,
        in_specs=[hbm] * 5,
        out_specs=[vmem] * 5,
        scratch_shapes=[
            f32(SLAB, COLS),
            f32(NZ, SLAB, CA),
            f32(NH, 12, ROWS, CB),
            f32(NZ, SLAB, CA),
            f32(NH, NZ, ROWS, CB),
            f32(2, HALF, SLAB, CA),
            f32(2, HALF, ROWS, CB),
            f32(2, NZ, ROWS, CB),
            f32(NZ, ROWS, CB),
            f32(2, HALF, ROWS, CB),
            f32(SLAB, CA),
            f32(2, 16, CA),
            f32(2, ROWS, CA),
            f32(256, COLS),
            f32(2, 64, 256),
            f32(2, 64, COLS),
            f32(NZ, 2, 2, 64, 128),
            f32(NZ, 2, 64, 128),
            f32(NZ, 64, 128),
            f32(256, 1536), f32(256, COLS), f32(ROWS, COLS), f32(ROWS, COLS), f32(ROWS, COLS),
            pltpu.VMEM((256, 1536), BF16),
            pltpu.VMEM((256, 1536), BF16),
            pltpu.VMEM((256, 3 * COLS), BF16),
            dma((5,)),
            dma((SENDS,)), dma((ARRIVALS,)),
            dma((NZ,)), dma((1,)),
        ],
        compiler_params=pltpu.CompilerParams(
            collective_id=0, has_side_effects=True, vmem_limit_bytes=48 << 20
        ),
        name="step",
    )(*[pltpu.with_memory_space_constraint(a, pltpu.HBM) for a in (inputs, out_grad, weight, moment_mean, moment_square)])
    return pl.pallas_call(
        write,
        out_shape=results,
        in_specs=[vmem] * 5,
        out_specs=[pl.BlockSpec(memory_space=pltpu.HBM)] * 5,
        scratch_shapes=[dma((5,))],
        compiler_params=pltpu.CompilerParams(vmem_limit_bytes=1 << 20),
        name="write",
    )(*done)


def solution(mesh):
    split = Mesh(mesh.devices.reshape(NZ, NH, NX, 2, 2), ("z", "h", "x", "l", "c"))
    tile = P(("x", "z", "h"), ("l", "c"))
    return jax.shard_map(
        per_device,
        mesh=split,
        in_specs=(P(("z", "h"), "x"), P(("z", "h"), ("l", "c")), tile, tile, tile),
        out_specs=(P(("z", "h", "x"), ("l", "c")), P(("z", "h", "l", "c"), "x"), tile, tile, tile),
        check_vma=False,
    )
```
